256 devices in a mesh: ty: 8 (over z_hi, y), tx: 32 (over z_lo, x, core).
Axes of the slice: x: 4, y: 4, z: 8 (z_hi: 2, z_lo: 4; z = z_hi * 4 + z_lo), core: 2. Of those that a mesh axis runs over, the one named last changes fastest.
Arguments:
- tracer_start: float32 [48, 128, 4096], P(None, 'ty', 'tx'), may hold values from -6 to 6
- observed: bfloat16 [48, 128, 4096], P(None, 'ty', 'tx'), may hold values from -6 to 6
- east_speed: bfloat16 [48, 128, 4096], P(None, 'ty', 'tx'), may hold values from -4 to 4
- north_speed: bfloat16 [48, 128, 4096], P(None, 'ty', 'tx'), may hold values from -4 to 4
- mixing: bfloat16 [48, 128, 4096], P(None, 'ty', 'tx'), may hold values from 0.019897461 to 0.19921875
- vertical_mixing: bfloat16 [47, 128, 4096], P(None, 'ty', 'tx'), may hold values from 0.19921875 to 5
- relax_rate: bfloat16 [48, 128, 4096], P(None, 'ty', 'tx'), may hold values from 0.049804688 to 0.5
- level_count: int32 [128, 4096], P('ty', 'tx'), may hold values from 0 to 48, as said below
- face_east: int32 [128, 4096], P('ty', 'tx'), may hold values from 0 to 48, as said below
- face_north: int32 [128, 4096], P('ty', 'tx'), may hold values from 0 to 48, as said below
Outputs:
- adjoint_start: float32 [48, 128, 4096], P(None, 'ty', 'tx')
- mixing_gradient: float32 [48, 128, 4096], P(None, 'ty', 'tx')
The draws below stay inside these ranges and needn't reach their ends.
Inputs may be any that keep to these rules, and one draw needn't show every extreme that they name: Levels 0 to level_count - 1 of a column are water; 0 marks land. `face_east`: the smaller of the level counts of a column and of the next column east, the last column's next being the first. `face_north`: the smaller of the level counts of a column and of the next row's column north, the last row's next being the first.
All inputs are finite; a program needn't handle non-finite values.
Results may differ from the reference program's by a relative error of at most 0.0006.
Values sent between devices are 32-bit elements; how exact they have to be, the bound alone decides.
A program may use at most 64 MiB of HBM per device.

```python
import math
import jax
import jax.numpy as jnp
from jax import lax

L = 48
NY = 128
NX = 4096


def level_tables(key):
    base = jax.random.fold_in(key, 11)
    key_land, key_depth = jax.random.split(base)
    land_cells = jax.random.randint(key_land, (NY, NX), 0, 5) == 0
    depths = jax.random.randint(key_depth, (NY, NX), 1, L + 1)
    counts = jnp.where(land_cells, 0, depths).astype(jnp.int32)
    counts = counts.at[0, 0].set(L).at[0, 1].set(L).at[1, 0].set(L).at[0, 2].set(0)
    east_levels = jnp.minimum(counts, jnp.roll(counts, -1, axis=1))
    north_levels = jnp.minimum(counts, jnp.roll(counts, -1, axis=0))
    return (counts, east_levels.astype(jnp.int32), north_levels.astype(jnp.int32))


def draw_level_count(key, part):
    return level_tables(key)[0]


def draw_face_east(key, part):
    return level_tables(key)[1]


def draw_face_north(key, part):
    return level_tables(key)[2]


def block_levels(rng, extent, cuts, smallest, largest):
    level = 1.0
    for position, blocks in cuts:
        draws = jax.random.uniform(jax.random.fold_in(jax.random.fold_in(rng, 6), position), (blocks,), jnp.float32, smallest / len(cuts), largest / len(cuts))
        level = level * jnp.repeat(jnp.exp(draws), extent[position] // blocks).reshape((-1,) + (1,) * (len(extent) - 1 - position))
    return level


def bell_draw(own_key, shape, deviation, limit, cuts=(), dtype=jnp.bfloat16):
    drawn = jax.random.normal(own_key, shape, jnp.float32) * deviation
    if len(cuts) > 0:
        drawn = block_levels(own_key, shape, cuts, -0.22, 0.18) * drawn
    return jnp.clip(drawn, min=-limit, max=limit).astype(dtype)


def setup_inputs(seed: int = 0) -> dict:
    keys = jax.random.split(jax.random.key(seed), 11)
    tracer_start = bell_draw(keys[0], (L, NY, NX), 1.0, 6.0, ((1, 8), (2, 32)), jnp.float32)
    observed = bell_draw(keys[1], (L, NY, NX), 1.0, 6.0, ((1, 8), (2, 32)))
    east_speed = bell_draw(keys[2], (L, NY, NX), 0.3, 4.0, ((1, 8), (2, 32)))
    north_speed = bell_draw(keys[3], (L, NY, NX), 0.3, 4.0, ((1, 8), (2, 32)))
    mixing = jnp.clip(jnp.exp(math.log(0.19921875) - 2.3038113 * jax.random.uniform(keys[4], (L, NY, NX), jnp.float32) ** block_levels(keys[4], (L, NY, NX), ((1, 8), (2, 32)), -0.2, 0.2)), 0.019897461, 0.19921875).astype(jnp.bfloat16)
    vertical_mixing = jnp.clip(jnp.exp(math.log(5.0) - 3.2227897 * jax.random.uniform(keys[5], (L - 1, NY, NX), jnp.float32) ** block_levels(keys[5], (L - 1, NY, NX), ((1, 8), (2, 32)), -0.2, 0.2)), 0.19921875, 5.0).astype(jnp.bfloat16)
    relax_rate = jnp.clip(jnp.exp(math.log(0.5) - 2.306499 * jax.random.uniform(keys[6], (L, NY, NX), jnp.float32) ** block_levels(keys[6], (L, NY, NX), ((1, 8), (2, 32)), -0.2, 0.2)), 0.049804688, 0.5).astype(jnp.bfloat16)
    level_count = draw_level_count(jax.random.fold_in(keys[10], 71), 0)
    face_east = draw_face_east(jax.random.fold_in(keys[10], 71), 0)
    face_north = draw_face_north(jax.random.fold_in(keys[10], 71), 0)
    return {"tracer_start": tracer_start, "observed": observed, "east_speed": east_speed, "north_speed": north_speed, "mixing": mixing, "vertical_mixing": vertical_mixing, "relax_rate": relax_rate, "level_count": level_count, "face_east": face_east, "face_north": face_north}


def solve_columns(rhs, level_links):
    levels = rhs.shape[0]
    nothing = jnp.zeros_like(rhs[0])
    ratios = []
    carries = []
    last_ratio = nothing
    last_carry = nothing
    for height in range(levels):
        upper_link = level_links[height - 1] if height > 0 else nothing
        lower_link = level_links[height] if height < levels - 1 else nothing
        divisor = 1.0 + upper_link + lower_link - upper_link * last_ratio
        last_carry = (rhs[height] + upper_link * last_carry) / divisor
        last_ratio = lower_link / divisor
        ratios.append(last_ratio)
        carries.append(last_carry)
    result = [carries[-1]]
    for height in range(levels - 2, -1, -1):
        result.append(carries[height] + ratios[height] * result[-1])
    return jnp.stack(result[::-1], axis=0)


def mask_levels(level_total, counts):
    heights = lax.broadcasted_iota(jnp.int32, (level_total,) + counts.shape, 0)
    return (heights < counts[None]).astype(jnp.float32)


def reference(tracer_start, observed, east_speed, north_speed, mixing, vertical_mixing, relax_rate, level_count, face_east, face_north):
    water = mask_levels(L, level_count)
    open_east = mask_levels(L, face_east)
    open_north = mask_levels(L, face_north)
    diffusion = mixing.astype(jnp.float32)
    speed_east = east_speed.astype(jnp.float32)
    speed_north = north_speed.astype(jnp.float32)
    east_minus = open_east * (0.5 * speed_east - diffusion)
    east_plus = open_east * (0.5 * speed_east + diffusion)
    north_minus = open_north * (0.5 * speed_north - diffusion)
    north_plus = open_north * (0.5 * speed_north + diffusion)
    level_links = vertical_mixing.astype(jnp.float32) * water[:-1] * water[1:]
    sink_rate = water * relax_rate.astype(jnp.float32)

    def advance(state):
        flux_east = east_plus * state + east_minus * jnp.roll(state, -1, 2)
        flux_north = north_plus * state + north_minus * jnp.roll(state, -1, 1)
        spread = (flux_east - jnp.roll(flux_east, 1, 2)) + (flux_north - jnp.roll(flux_north, 1, 1))
        return solve_columns(state - spread - sink_rate * jnp.tanh(state), level_links)

    def retreat(adjoint, state):
        solved = solve_columns(adjoint, level_links)
        grad_east = jnp.roll(solved, -1, 2) - solved
        grad_north = jnp.roll(solved, -1, 1) - solved
        squeeze = jnp.tanh(state)
        new_adjoint = solved * (1.0 - sink_rate * (1.0 - squeeze * squeeze))
        new_adjoint = new_adjoint + east_plus * grad_east + jnp.roll(east_minus * grad_east, 1, 2)
        new_adjoint = new_adjoint + north_plus * grad_north + jnp.roll(north_minus * grad_north, 1, 1)
        kappa_part = -(open_east * grad_east * (jnp.roll(state, -1, 2) - state) + open_north * grad_north * (jnp.roll(state, -1, 1) - state))
        return new_adjoint, kappa_part

    middle = advance(tracer_start)
    final_state = advance(middle)
    adjoint = water * (final_state - observed.astype(jnp.float32))
    adjoint, late_part = retreat(adjoint, middle)
    adjoint, early_part = retreat(adjoint, tracer_start)
    return adjoint, late_part + early_part
```

```python
import functools

import jax
import jax.numpy as jnp
from jax import lax
from jax.experimental import pallas as pl
from jax.experimental.pallas import tpu as pltpu
from jax.sharding import PartitionSpec as P

EAST, WEST, NORTH, SOUTH = range(4)
UNROLL = 4
CHAIN_UNROLL = 8


def kernel(
    sizes,
    tracer_hbm, observed_hbm, east_hbm, north_hbm, mixing_hbm, vertical_hbm, relax_hbm,
    count_hbm, face_east_hbm, face_north_hbm,
    adjoint_hbm, gradient_hbm,
    start, observed, east, north, mixing, vertical, relax, count, face_east, face_north,
    east_minus, east_plus, north_minus, north_plus, sink,
    inverse, ratio, feed,
    middle, rhs, carry, solved_two, solved_one, gradient,
    to_east0, to_north0, to_west0, to_south0,
    to_east, to_west, to_north, to_south,
    from_west0, from_south0, from_east0, from_north0,
    from_west, from_east, from_south, from_north,
    load_sem, store_sem, send_sem, recv_sem,
):
    levels, rows, lanes, size_y, size_x = sizes
    my_y = lax.axis_index("ty")
    my_x = lax.axis_index("tx")
    neighbour = {
        EAST: {"tx": lax.rem(my_x + 1, size_x)},
        WEST: {"tx": lax.rem(my_x + size_x - 1, size_x)},
        NORTH: {"ty": lax.rem(my_y + 1, size_y)},
        SOUTH: {"ty": lax.rem(my_y + size_y - 1, size_y)},
    }
    barrier = pltpu.get_barrier_semaphore()
    for side in range(4):
        pl.semaphore_signal(
            barrier, inc=1, device_id=neighbour[side], device_id_type=pl.DeviceIdType.MESH
        )

    loads = [
        pltpu.make_async_copy(source, target, load_sem.at[slot])
        for slot, (source, target) in enumerate(
            (
                (tracer_hbm, start),
                (east_hbm, east),
                (north_hbm, north),
                (mixing_hbm, mixing),
                (face_east_hbm, face_east),
                (face_north_hbm, face_north),
                (vertical_hbm, vertical),
                (count_hbm, count),
                (relax_hbm, relax),
                (observed_hbm, observed),
            )
        )
    ]
    for load in loads:
        load.start()
    for load in loads[:6]:
        load.wait()

    lane = lax.broadcasted_iota(jnp.int32, (rows, lanes), 1)
    row = lax.broadcasted_iota(jnp.int32, (rows, lanes), 0)
    first_lane, last_lane = lane == 0, lane == lanes - 1
    rim_lanes = first_lane | last_lane
    first_row, last_row = row == 0, row == rows - 1
    even_lane = lane % 2 == 0
    zero = jnp.zeros((rows, lanes), jnp.float32)

    def at(height):
        return pl.ds(pl.multiple_of(height * rows, rows), rows)

    def from_lane_east(block):
        return jnp.where(last_lane, 0.0, pltpu.roll(block, lanes - 1, 1))

    def from_lane_west(block):
        return jnp.where(first_lane, 0.0, pltpu.roll(block, 1, 1))

    def from_row_north(block):
        return jnp.where(last_row, 0.0, pltpu.roll(block, rows - 1, 0))

    def from_row_south(block):
        return jnp.where(first_row, 0.0, pltpu.roll(block, 1, 0))

    def pack(packed, block, height):
        turned = pltpu.roll(block, 2 * height, 1)
        mine = ((lane + 1) % lanes) // 2 == height
        return jnp.where(mine, turned, packed)

    def unpack(packed, height):
        return jnp.where(rim_lanes, pltpu.roll(packed, lax.rem(lanes - 2 * height, lanes), 1), 0.0)

    def south_row(ref):
        return ref[pl.ds(0, levels, stride=rows), :]

    def north_row(ref):
        return ref[pl.ds(rows - 1, levels, stride=rows), :]

    def add_rows(ref, south, north):
        low = pl.ds(0, levels, stride=rows)
        high = pl.ds(rows - 1, levels, stride=rows)
        ref[low, :] = ref[low, :] + south
        ref[high, :] = ref[high, :] + north

    def loop(body, init, unroll=UNROLL):
        return lax.fori_loop(0, levels, body, init, unroll=unroll)

    def remote(source, target, slot, side):
        return pltpu.make_async_remote_copy(
            src_ref=source,
            dst_ref=target,
            send_sem=send_sem.at[slot, side],
            recv_sem=recv_sem.at[slot, side],
            device_id=neighbour[side],
            device_id_type=pl.DeviceIdType.MESH,
        )

    open_to_east = face_east[...]
    open_to_north = face_north[...]

    def coefficients(height, packs):
        own = start[at(height), :]
        spread = mixing[height].astype(jnp.float32)
        half_east = 0.5 * east[height].astype(jnp.float32)
        half_north = 0.5 * north[height].astype(jnp.float32)
        is_east = height < open_to_east
        is_north = height < open_to_north
        minus = jnp.where(is_east, half_east - spread, 0.0)
        plus = jnp.where(is_east, half_east + spread, 0.0)
        east_minus[at(height), :] = minus
        east_plus[at(height), :] = plus
        north_minus[at(height), :] = jnp.where(is_north, half_north - spread, 0.0)
        north_plus[at(height), :] = jnp.where(is_north, half_north + spread, 0.0)
        return (
            pack(packs[0], own, height),
            pack(packs[1], minus, height),
            pack(packs[2], plus, height),
        )

    start_pack, minus_pack, plus_pack = loop(coefficients, (zero, zero, zero))
    minus_row = north_row(north_minus)
    plus_row = north_row(north_plus)
    to_east0[0] = plus_pack * start_pack
    to_east0[1] = minus_pack
    to_west0[...] = start_pack
    to_north0[0] = plus_row * north_row(start)
    to_north0[1] = minus_row
    to_south0[...] = south_row(start)

    first = {
        NORTH: remote(to_north0, from_south0, 0, NORTH),
        SOUTH: remote(to_south0, from_north0, 0, SOUTH),
        EAST: remote(to_east0, from_west0, 0, EAST),
        WEST: remote(to_west0, from_east0, 0, WEST),
    }
    exchanges = [first] + [
        {
            NORTH: remote(to_north.at[slot], from_south.at[slot], slot + 1, NORTH),
            SOUTH: remote(to_south.at[slot], from_north.at[slot], slot + 1, SOUTH),
            EAST: remote(to_east.at[slot], from_west.at[slot], slot + 1, EAST),
            WEST: remote(to_west.at[slot], from_east.at[slot], slot + 1, WEST),
        }
        for slot in range(3)
    ]

    def send(turn):
        for side in (NORTH, SOUTH, EAST, WEST):
            exchanges[turn][side].start()

    def receive(turn):
        for side in (EAST, WEST, NORTH, SOUTH):
            exchanges[turn][side].wait_recv()

    pl.semaphore_wait(barrier, 4)
    send(0)

    for load in loads[6:]:
        load.wait()
    wet = count[...]

    def factor(height, last):
        last_ratio, upper = last
        lower = jnp.where(
            height + 1 < wet, vertical[jnp.minimum(height, levels - 2)].astype(jnp.float32), 0.0
        )
        lower = jnp.where(height < levels - 1, lower, 0.0)
        inverted = 1.0 / (1.0 + upper + lower - upper * last_ratio)
        following = lower * inverted
        inverse[at(height), :] = inverted
        ratio[at(height), :] = following
        feed[at(height), :] = upper * inverted
        return following, lower

    loop(factor, (zero, zero), CHAIN_UNROLL)

    def step_inside(state):
        def body(height, nothing):
            own = state[at(height), :]
            plus_x, minus_x = east_plus[at(height), :], east_minus[at(height), :]
            plus_y, minus_y = north_plus[at(height), :], north_minus[at(height), :]
            flux_x = plus_x * own + minus_x * from_lane_east(own)
            flux_y = plus_y * own + minus_y * from_row_north(own)
            spread = (flux_x - from_lane_west(flux_x)) + (flux_y - from_row_south(flux_y))
            rate = sink[at(height), :]
            rhs[at(height), :] = own - spread - rate * jnp.tanh(own)
            return nothing

        loop(body, 0)

    def sink_rates(height, nothing):
        sink[at(height), :] = jnp.where(height < wet, relax[height].astype(jnp.float32), 0.0)
        return nothing

    loop(sink_rates, 0)
    step_inside(start)

    def eliminate(rim):
        def body(height, last):
            right = rhs[at(height), :] + unpack(rim, height)
            new = right * inverse[at(height), :] + feed[at(height), :] * last
            carry[at(height), :] = new
            return new

        loop(body, zero, CHAIN_UNROLL)

    def substitute(visit, init):
        def body(step, state):
            height = levels - 1 - step
            last, kept = state
            new = carry[at(height), :] + ratio[at(height), :] * last
            return new, visit(height, new, kept)

        return loop(body, (zero, init), CHAIN_UNROLL)[1]

    def solve_into(target):
        def visit(height, value, packed):
            target[at(height), :] = value
            return pack(packed, value, height)

        return substitute(visit, zero)

    def to_even(packed):
        return pltpu.roll(packed, 1, 1)

    def to_odd(packed):
        return pltpu.roll(packed, lanes - 1, 1)

    def step_rims(state, state_pack, west_product, east_state, south_product, north_state):
        add_rows(rhs, south_product + south_minus * south_row(state), -minus_row * north_state)
        return jnp.where(
            even_lane, to_even(west_product) + west_minus * state_pack, -minus_pack * to_odd(east_state)
        )

    receive(0)
    west_minus = to_even(from_west0[1])
    south_minus = from_south0[1]
    rim = step_rims(
        start, start_pack, from_west0[0], from_east0[...], from_south0[0], from_north0[...]
    )
    eliminate(rim)
    middle_pack = solve_into(middle)
    to_north[0] = plus_row * north_row(middle)
    to_south[0] = south_row(middle)
    to_east[0] = plus_pack * middle_pack
    to_west[0] = middle_pack
    send(1)
    step_inside(middle)
    receive(1)
    rim = step_rims(middle, middle_pack, from_west[0], from_east[0], from_south[0], from_north[0])
    eliminate(rim)

    def misfit(height, value, nothing):
        seen = observed[height].astype(jnp.float32)
        rhs[at(height), :] = jnp.where(height < wet, value - seen, 0.0)
        return nothing

    substitute(misfit, 0)
    eliminate(zero)
    two_pack = solve_into(solved_two)
    to_north[1] = north_row(solved_two)
    to_south[1] = south_row(solved_two)
    to_east[1] = two_pack
    to_west[1] = two_pack
    send(2)

    def adjoint_inside(solved, state, target, with_gradient):
        def body(height, nothing):
            own = solved[at(height), :]
            value = state[at(height), :]
            slope_x = from_lane_east(own) - own
            slope_y = from_row_north(own) - own
            squeeze = jnp.tanh(value)
            total = own * (1.0 - sink[at(height), :] * (1.0 - squeeze * squeeze))
            total = total + east_plus[at(height), :] * slope_x
            total = total + from_lane_west(east_minus[at(height), :] * slope_x)
            total = total + north_plus[at(height), :] * slope_y
            total = total + from_row_south(north_minus[at(height), :] * slope_y)
            target[at(height), :] = total
            if with_gradient:
                gradient_inside(height, slope_x, slope_y, value, True)
            return nothing

        loop(body, 0)

    def gradient_inside(height, slope_x, slope_y, value, more):
        rise_x = pltpu.roll(value, lanes - 1, 1) - value
        rise_y = pltpu.roll(value, rows - 1, 0) - value
        inner_x = (height < open_to_east) & (lane < lanes - 1)
        inner_y = (height < open_to_north) & (row < rows - 1)
        part = jnp.where(inner_x, slope_x * rise_x, 0.0) + jnp.where(inner_y, slope_y * rise_y, 0.0)
        if more:
            gradient[at(height), :] = gradient[at(height), :] - part
        else:
            gradient[at(height), :] = -part

    lane_level = ((lane + 1) % lanes) // 2
    odd_open = (lane_level < open_to_east[:, lanes - 1 :]) & (lane % 2 == 1)
    row_level = lax.broadcasted_iota(jnp.int32, (levels, lanes), 0)
    row_open = row_level < open_to_north[rows - 1 :, :]

    def gradient_rims(solved, solved_pack, state, state_pack, solved_east, state_east, solved_north, state_north):
        packed = (to_odd(solved_east) - solved_pack) * (to_odd(state_east) - state_pack)
        lined = (solved_north - north_row(solved)) * (state_north - north_row(state))
        return jnp.where(odd_open, -packed, 0.0), jnp.where(row_open, -lined, 0.0)

    def adjoint_rims(solved, solved_pack, turn, target):
        add_rows(
            target,
            south_minus * (south_row(solved) - from_south[turn]),
            plus_row * from_north[turn],
        )
        return jnp.where(
            even_lane,
            west_minus * (solved_pack - to_even(from_west[turn])),
            plus_pack * to_odd(from_east[turn]),
        )

    adjoint_inside(solved_two, middle, rhs, False)
    receive(2)
    rim = adjoint_rims(solved_two, two_pack, 1, rhs)
    eliminate(rim)
    one_pack = solve_into(solved_one)
    to_north[2] = north_row(solved_one)
    to_south[2] = south_row(solved_one)
    to_east[2] = one_pack
    to_west[2] = one_pack
    send(3)

    late_rim, late_row = gradient_rims(
        solved_two, two_pack, middle, middle_pack,
        from_east[1], from_east[0], from_north[1], from_north[0],
    )

    def late_gradient(height, nothing):
        own = solved_two[at(height), :]
        slope_x = pltpu.roll(own, lanes - 1, 1) - own
        slope_y = pltpu.roll(own, rows - 1, 0) - own
        gradient_inside(height, slope_x, slope_y, middle[at(height), :], False)
        return nothing

    loop(late_gradient, 0)
    adjoint_inside(solved_one, start, rhs, True)
    receive(3)
    rim = adjoint_rims(solved_one, one_pack, 2, rhs)
    early_rim, early_row = gradient_rims(
        solved_one, one_pack, start, start_pack,
        from_east[2], from_east0[...], from_north[2], from_north0[...],
    )
    add_rows(gradient, jnp.zeros_like(early_row), late_row + early_row)
    gradient_rim = late_rim + early_rim

    def finish(height, nothing):
        rhs[at(height), :] = rhs[at(height), :] + unpack(rim, height)
        gradient[at(height), :] = gradient[at(height), :] + unpack(gradient_rim, height)
        return nothing

    loop(finish, 0)
    stores = [
        pltpu.make_async_copy(rhs, adjoint_hbm, store_sem.at[0]),
        pltpu.make_async_copy(gradient, gradient_hbm, store_sem.at[1]),
    ]
    for store in stores:
        store.start()
    for exchange in exchanges:
        for side in range(4):
            exchange[side].wait_send()
    for store in stores:
        store.wait()


def per_device(sizes, tracer_start, *others):
    levels, rows, lanes, _, _ = sizes
    flat = (levels * rows, lanes)
    field = pltpu.VMEM(flat, jnp.float32)
    columns = pltpu.VMEM((rows, lanes), jnp.float32)
    lines = pltpu.VMEM((levels, lanes), jnp.float32)

    def several(count, shape):
        return pltpu.VMEM((count,) + shape, jnp.float32)

    column, line = (rows, lanes), (levels, lanes)
    scratch = [field]
    scratch += [pltpu.VMEM(other.shape, other.dtype) for other in others]
    scratch += [field] * 14
    scratch += [several(2, column), several(2, line), columns, lines]
    scratch += [several(3, column), several(3, column), several(3, line), several(3, line)]
    scratch += [several(2, column), several(2, line), columns, lines]
    scratch += [several(3, column), several(3, column), several(3, line), several(3, line)]
    scratch += [
        pltpu.SemaphoreType.DMA((10,)),
        pltpu.SemaphoreType.DMA((2,)),
        pltpu.SemaphoreType.DMA((4, 4)),
        pltpu.SemaphoreType.DMA((4, 4)),
    ]
    out = jax.ShapeDtypeStruct(flat, jnp.float32)
    adjoint, gradient = pl.pallas_call(
        functools.partial(kernel, sizes),
        out_shape=(out, out),
        in_specs=[pl.BlockSpec(memory_space=pl.ANY)] * 10,
        out_specs=(pl.BlockSpec(memory_space=pl.ANY),) * 2,
        scratch_shapes=scratch,
        compiler_params=pltpu.CompilerParams(collective_id=0, has_side_effects=True),
    )(tracer_start.reshape(flat), *others)
    return adjoint.reshape(tracer_start.shape), gradient.reshape(tracer_start.shape)


def solution(mesh):
    block = P(None, "ty", "tx")
    plane = P("ty", "tx")
    size_y, size_x = mesh.shape["ty"], mesh.shape["tx"]

    def program(tracer_start, *others):
        levels, all_rows, all_lanes = tracer_start.shape
        sizes = (levels, all_rows // size_y, all_lanes // size_x, size_y, size_x)
        return jax.shard_map(
            functools.partial(per_device, sizes),
            mesh=mesh,
            in_specs=(block,) * 7 + (plane,) * 3,
            out_specs=(block, block),
            check_vma=False,
        )(tracer_start, *others)

    return program
```

```python
import functools

import jax
import jax.numpy as jnp
from jax import lax
from jax.experimental import pallas as pl
from jax.experimental.pallas import tpu as pltpu
from jax.sharding import PartitionSpec as P

EAST, WEST, NORTH, SOUTH = range(4)
UNROLL = 16
CHAIN_UNROLL = 48
PIECES = 4
VMEM_LIMIT = 16 * 1024 * 1024


def kernel(
    sizes,
    tracer_hbm, observed_hbm, east_hbm, north_hbm, mixing_hbm, vertical_hbm, relax_hbm,
    count_hbm, face_east_hbm, face_north_hbm,
    inside, gradient, result_rims,
    start, observed, east, north, mixing, vertical, relax, count, face_east, face_north,
    east_minus, east_plus, north_minus, north_plus, sink,
    inverse, ratio, feed,
    middle, rhs, carry, solved_two, solved_one,
    to_east0, to_north0, to_west0, to_south0,
    to_east, to_west, to_north, to_south,
    from_west0, from_south0, from_east0, from_north0,
    from_west, from_east, from_south, from_north,
    load_sem, send_sem, recv_sem,
):
    levels, rows, lanes, size_y, size_x = sizes
    my_y = lax.axis_index("ty")
    my_x = lax.axis_index("tx")
    neighbour = {
        EAST: {"tx": lax.rem(my_x + 1, size_x)},
        WEST: {"tx": lax.rem(my_x + size_x - 1, size_x)},
        NORTH: {"ty": lax.rem(my_y + 1, size_y)},
        SOUTH: {"ty": lax.rem(my_y + size_y - 1, size_y)},
    }
    barrier = pltpu.get_barrier_semaphore()
    for side in range(4):
        pl.semaphore_signal(
            barrier, inc=1, device_id=neighbour[side], device_id_type=pl.DeviceIdType.MESH
        )

    loads = [
        pltpu.make_async_copy(source, target, load_sem.at[slot])
        for slot, (source, target) in enumerate(
            (
                (tracer_hbm, start),
                (east_hbm, east),
                (north_hbm, north),
                (mixing_hbm, mixing),
                (face_east_hbm, face_east),
                (face_north_hbm, face_north),
                (vertical_hbm, vertical),
                (count_hbm, count),
                (relax_hbm, relax),
                (observed_hbm, observed),
            )
        )
    ]
    for load in loads:
        load.start()
    for load in loads[:6]:
        load.wait()

    lane = lax.broadcasted_iota(jnp.int32, (rows, lanes), 1)
    row = lax.broadcasted_iota(jnp.int32, (rows, lanes), 0)
    first_lane, last_lane = lane == 0, lane == lanes - 1
    rim_lanes = first_lane | last_lane
    first_row, last_row = row == 0, row == rows - 1
    even_lane = lane % 2 == 0
    zero = jnp.zeros((rows, lanes), jnp.float32)

    def at(height):
        return pl.ds(pl.multiple_of(height * rows, rows), rows)

    def from_lane_east(block):
        return jnp.where(last_lane, 0.0, pltpu.roll(block, lanes - 1, 1))

    def from_lane_west(block):
        return jnp.where(first_lane, 0.0, pltpu.roll(block, 1, 1))

    def from_row_north(block):
        return jnp.where(last_row, 0.0, pltpu.roll(block, rows - 1, 0))

    def from_row_south(block):
        return jnp.where(first_row, 0.0, pltpu.roll(block, 1, 0))

    def pack(packed, block, height):
        turned = pltpu.roll(block, 2 * height, 1)
        mine = ((lane + 1) % lanes) // 2 == height
        return jnp.where(mine, turned, packed)

    def unpack(packed, height):
        return jnp.where(rim_lanes, pltpu.roll(packed, lax.rem(lanes - 2 * height, lanes), 1), 0.0)

    def south_row(ref):
        return ref[pl.ds(0, levels, stride=rows), :]

    def north_row(ref):
        return ref[pl.ds(rows - 1, levels, stride=rows), :]

    def add_rows(ref, south, north):
        low = pl.ds(0, levels, stride=rows)
        high = pl.ds(rows - 1, levels, stride=rows)
        ref[low, :] = ref[low, :] + south
        ref[high, :] = ref[high, :] + north

    def loop(body, init, unroll=UNROLL):
        return lax.fori_loop(0, levels, body, init, unroll=unroll)

    def remote(source, target, slot, side):
        return pltpu.make_async_remote_copy(
            src_ref=source,
            dst_ref=target,
            send_sem=send_sem.at[slot, side],
            recv_sem=recv_sem.at[slot, side],
            device_id=neighbour[side],
            device_id_type=pl.DeviceIdType.MESH,
        )

    open_to_east = face_east[...]
    open_to_north = face_north[...]

    def coefficients(height, packs):
        own = start[at(height), :]
        spread = mixing[height].astype(jnp.float32)
        half_east = 0.5 * east[height].astype(jnp.float32)
        half_north = 0.5 * north[height].astype(jnp.float32)
        is_east = height < open_to_east
        is_north = height < open_to_north
        minus = jnp.where(is_east, half_east - spread, 0.0)
        plus = jnp.where(is_east, half_east + spread, 0.0)
        east_minus[at(height), :] = minus
        east_plus[at(height), :] = plus
        north_minus[at(height), :] = jnp.where(is_north, half_north - spread, 0.0)
        north_plus[at(height), :] = jnp.where(is_north, half_north + spread, 0.0)
        return (
            pack(packs[0], own, height),
            pack(packs[1], minus, height),
            pack(packs[2], plus, height),
        )

    start_pack, minus_pack, plus_pack = loop(coefficients, (zero, zero, zero))
    minus_row = north_row(north_minus)
    plus_row = north_row(north_plus)
    to_east0[0] = plus_pack * start_pack
    to_east0[1] = minus_pack
    to_west0[...] = start_pack
    to_north0[0] = plus_row * north_row(start)
    to_north0[1] = minus_row
    to_south0[...] = south_row(start)

    first = {
        NORTH: remote(to_north0, from_south0, 0, NORTH),
        SOUTH: remote(to_south0, from_north0, 0, SOUTH),
        EAST: remote(to_east0, from_west0, 0, EAST),
        WEST: remote(to_west0, from_east0, 0, WEST),
    }
    exchanges = [first] + [
        {
            NORTH: remote(to_north.at[slot], from_south.at[slot], slot + 1, NORTH),
            SOUTH: remote(to_south.at[slot], from_north.at[slot], slot + 1, SOUTH),
            EAST: remote(to_east.at[slot], from_west.at[slot], slot + 1, EAST),
            WEST: remote(to_west.at[slot], from_east.at[slot], slot + 1, WEST),
        }
        for slot in range(3)
    ]

    def send(turn):
        for side in (NORTH, SOUTH, EAST, WEST):
            exchanges[turn][side].start()

    def receive(turn):
        for side in (EAST, WEST, NORTH, SOUTH):
            exchanges[turn][side].wait_recv()

    pl.semaphore_wait(barrier, 4)
    send(0)

    for load in loads[6:]:
        load.wait()
    wet = count[...]

    def factor(height, last):
        last_ratio, upper = last
        lower = jnp.where(
            height + 1 < wet, vertical[jnp.minimum(height, levels - 2)].astype(jnp.float32), 0.0
        )
        lower = jnp.where(height < levels - 1, lower, 0.0)
        inverted = 1.0 / (1.0 + upper + lower - upper * last_ratio)
        following = lower * inverted
        inverse[at(height), :] = inverted
        ratio[at(height), :] = following
        feed[at(height), :] = upper * inverted
        return following, lower

    loop(factor, (zero, zero), CHAIN_UNROLL)

    def step_inside(state):
        def body(height, nothing):
            own = state[at(height), :]
            plus_x, minus_x = east_plus[at(height), :], east_minus[at(height), :]
            plus_y, minus_y = north_plus[at(height), :], north_minus[at(height), :]
            flux_x = plus_x * own + minus_x * from_lane_east(own)
            flux_y = plus_y * own + minus_y * from_row_north(own)
            spread = (flux_x - from_lane_west(flux_x)) + (flux_y - from_row_south(flux_y))
            rate = sink[at(height), :]
            rhs[at(height), :] = own - spread - rate * jnp.tanh(own)
            return nothing

        loop(body, 0)

    def sink_rates(height, nothing):
        sink[at(height), :] = jnp.where(height < wet, relax[height].astype(jnp.float32), 0.0)
        return nothing

    loop(sink_rates, 0)
    step_inside(start)

    def eliminate(rim):
        def body(height, last):
            right = rhs[at(height), :] + unpack(rim, height)
            new = right * inverse[at(height), :] + feed[at(height), :] * last
            carry[at(height), :] = new
            return new

        loop(body, zero, CHAIN_UNROLL)

    def substitute(visit, init):
        def body(step, state):
            height = levels - 1 - step
            last, kept = state
            new = carry[at(height), :] + ratio[at(height), :] * last
            return new, visit(height, new, kept)

        return loop(body, (zero, init), CHAIN_UNROLL)[1]

    def solve_into(target):
        def visit(height, value, packed):
            target[at(height), :] = value
            return pack(packed, value, height)

        return substitute(visit, zero)

    def to_even(packed):
        return pltpu.roll(packed, 1, 1)

    def to_odd(packed):
        return pltpu.roll(packed, lanes - 1, 1)

    def step_rims(state, state_pack, west_product, east_state, south_product, north_state):
        add_rows(rhs, south_product + south_minus * south_row(state), -minus_row * north_state)
        return jnp.where(
            even_lane, to_even(west_product) + west_minus * state_pack, -minus_pack * to_odd(east_state)
        )

    receive(0)
    west_minus = to_even(from_west0[1])
    south_minus = from_south0[1]
    rim = step_rims(
        start, start_pack, from_west0[0], from_east0[...], from_south0[0], from_north0[...]
    )
    eliminate(rim)
    middle_pack = solve_into(middle)
    to_north[0] = plus_row * north_row(middle)
    to_south[0] = south_row(middle)
    to_east[0] = plus_pack * middle_pack
    to_west[0] = middle_pack
    send(1)
    step_inside(middle)
    receive(1)
    rim = step_rims(middle, middle_pack, from_west[0], from_east[0], from_south[0], from_north[0])
    eliminate(rim)

    def misfit(height, value, nothing):
        seen = observed[height].astype(jnp.float32)
        rhs[at(height), :] = jnp.where(height < wet, value - seen, 0.0)
        return nothing

    substitute(misfit, 0)
    eliminate(zero)
    two_pack = solve_into(solved_two)
    to_north[1] = north_row(solved_two)
    to_south[1] = south_row(solved_two)
    to_east[1] = two_pack
    to_west[1] = two_pack
    send(2)

    def adjoint_inside(solved, state, target, with_gradient):
        def body(height, nothing):
            own = solved[at(height), :]
            value = state[at(height), :]
            slope_x = from_lane_east(own) - own
            slope_y = from_row_north(own) - own
            squeeze = jnp.tanh(value)
            total = own * (1.0 - sink[at(height), :] * (1.0 - squeeze * squeeze))
            total = total + east_plus[at(height), :] * slope_x
            total = total + from_lane_west(east_minus[at(height), :] * slope_x)
            total = total + north_plus[at(height), :] * slope_y
            total = total + from_row_south(north_minus[at(height), :] * slope_y)
            target[at(height), :] = total
            if with_gradient:
                gradient_inside(height, slope_x, slope_y, value, True)
            return nothing

        loop(body, 0)

    def gradient_inside(height, slope_x, slope_y, value, more):
        rise_x = pltpu.roll(value, lanes - 1, 1) - value
        rise_y = pltpu.roll(value, rows - 1, 0) - value
        inner_x = (height < open_to_east) & (lane < lanes - 1)
        inner_y = (height < open_to_north) & (row < rows - 1)
        part = jnp.where(inner_x, slope_x * rise_x, 0.0) + jnp.where(inner_y, slope_y * rise_y, 0.0)
        if more:
            gradient[at(height), :] = gradient[at(height), :] - part
        else:
            gradient[at(height), :] = -part

    lane_level = ((lane + 1) % lanes) // 2
    odd_open = (lane_level < open_to_east[:, lanes - 1 :]) & (lane % 2 == 1)
    row_level = lax.broadcasted_iota(jnp.int32, (levels, lanes), 0)
    row_open = row_level < open_to_north[rows - 1 :, :]

    def gradient_rims(solved, solved_pack, state, state_pack, solved_east, state_east, solved_north, state_north):
        packed = (to_odd(solved_east) - solved_pack) * (to_odd(state_east) - state_pack)
        lined = (solved_north - north_row(solved)) * (state_north - north_row(state))
        return jnp.where(odd_open, -packed, 0.0), jnp.where(row_open, -lined, 0.0)

    def adjoint_rims(solved, solved_pack, turn, target):
        add_rows(
            target,
            south_minus * (south_row(solved) - from_south[turn]),
            plus_row * from_north[turn],
        )
        return jnp.where(
            even_lane,
            west_minus * (solved_pack - to_even(from_west[turn])),
            plus_pack * to_odd(from_east[turn]),
        )

    adjoint_inside(solved_two, middle, rhs, False)
    receive(2)
    rim = adjoint_rims(solved_two, two_pack, 1, rhs)
    eliminate(rim)
    one_pack = solve_into(solved_one)
    to_north[2] = north_row(solved_one)
    to_south[2] = south_row(solved_one)
    to_east[2] = one_pack
    to_west[2] = one_pack
    send(3)

    late_rim, late_row = gradient_rims(
        solved_two, two_pack, middle, middle_pack,
        from_east[1], from_east[0], from_north[1], from_north[0],
    )

    def late_gradient(height, nothing):
        own = solved_two[at(height), :]
        slope_x = pltpu.roll(own, lanes - 1, 1) - own
        slope_y = pltpu.roll(own, rows - 1, 0) - own
        gradient_inside(height, slope_x, slope_y, middle[at(height), :], False)
        return nothing

    loop(late_gradient, 0)
    adjoint_inside(solved_one, start, inside, True)
    receive(3)
    result_rims[0] = adjoint_rims(solved_one, one_pack, 2, inside)
    early_rim, early_row = gradient_rims(
        solved_one, one_pack, start, start_pack,
        from_east[2], from_east0[...], from_north[2], from_north0[...],
    )
    add_rows(gradient, jnp.zeros_like(early_row), late_row + early_row)
    result_rims[1] = late_rim + early_rim
    for exchange in exchanges:
        for side in range(4):
            exchange[side].wait_send()


def finish(sizes, inside, gradient_inside, rims, adjoint_hbm, gradient_hbm, adjoint, gradient, store_sem):
    levels, rows, lanes, _, _ = sizes
    lane = lax.broadcasted_iota(jnp.int32, (rows, lanes), 1)
    rim_lanes = (lane == 0) | (lane == lanes - 1)
    stores = []
    for piece in range(PIECES):
        first, last = piece * levels // PIECES, (piece + 1) * levels // PIECES
        for height in range(first, last):
            here = slice(height * rows, (height + 1) * rows)
            for slot, (source, target) in enumerate(((inside, adjoint), (gradient_inside, gradient))):
                rim = pltpu.roll(rims[slot], (lanes - 2 * height) % lanes, 1)
                target[here, :] = source[here, :] + jnp.where(rim_lanes, rim, 0.0)
        part = slice(first * rows, last * rows)
        for slot, (source, target) in enumerate(((adjoint, adjoint_hbm), (gradient, gradient_hbm))):
            store = pltpu.make_async_copy(
                source.at[part, :], target.at[part, :], store_sem.at[piece, slot]
            )
            store.start()
            stores.append(store)
    for store in stores:
        store.wait()


def per_device(sizes, tracer_start, *others):
    levels, rows, lanes, _, _ = sizes
    flat = (levels * rows, lanes)
    field = pltpu.VMEM(flat, jnp.float32)
    columns = pltpu.VMEM((rows, lanes), jnp.float32)
    lines = pltpu.VMEM((levels, lanes), jnp.float32)

    def several(count, shape):
        return pltpu.VMEM((count,) + shape, jnp.float32)

    column, line = (rows, lanes), (levels, lanes)
    scratch = [field]
    scratch += [pltpu.VMEM(other.shape, other.dtype) for other in others]
    scratch += [field] * 13
    scratch += [several(2, column), several(2, line), columns, lines]
    scratch += [several(3, column), several(3, column), several(3, line), several(3, line)]
    scratch += [several(2, column), several(2, line), columns, lines]
    scratch += [several(3, column), several(3, column), several(3, line), several(3, line)]
    scratch += [
        pltpu.SemaphoreType.DMA((10,)),
        pltpu.SemaphoreType.DMA((4, 4)),
        pltpu.SemaphoreType.DMA((4, 4)),
    ]
    out = jax.ShapeDtypeStruct(flat, jnp.float32)
    in_vmem = pl.BlockSpec(memory_space=pltpu.VMEM)
    in_hbm = pl.BlockSpec(memory_space=pl.ANY)
    parts = pl.pallas_call(
        functools.partial(kernel, sizes),
        out_shape=(out, out, jax.ShapeDtypeStruct((2,) + column, jnp.float32)),
        in_specs=[in_hbm] * 10,
        out_specs=(in_vmem,) * 3,
        scratch_shapes=scratch,
        compiler_params=pltpu.CompilerParams(collective_id=0, has_side_effects=True, vmem_limit_bytes=VMEM_LIMIT),
    )(*[pltpu.with_memory_space_constraint(a, pltpu.HBM) for a in (tracer_start.reshape(flat), *others)])
    adjoint, gradient = pl.pallas_call(
        functools.partial(finish, sizes),
        out_shape=(out, out),
        in_specs=[in_vmem] * 3,
        out_specs=(in_hbm,) * 2,
        scratch_shapes=[field, field, pltpu.SemaphoreType.DMA((PIECES, 2))],
        compiler_params=pltpu.CompilerParams(vmem_limit_bytes=VMEM_LIMIT),
    )(*parts)
    return adjoint.reshape(tracer_start.shape), gradient.reshape(tracer_start.shape)


def solution(mesh):
    block = P(None, "ty", "tx")
    plane = P("ty", "tx")
    size_y, size_x = mesh.shape["ty"], mesh.shape["tx"]

    def program(tracer_start, *others):
        levels, all_rows, all_lanes = tracer_start.shape
        sizes = (levels, all_rows // size_y, all_lanes // size_x, size_y, size_x)
        return jax.shard_map(
            functools.partial(per_device, sizes),
            mesh=mesh,
            in_specs=(block,) * 7 + (plane,) * 3,
            out_specs=(block, block),
            check_vma=False,
        )(tracer_start, *others)

    return program
```
